32 devices in a mesh: dp: 2 (over x), seq: 4 (over z), section: 4 (over y, core).
Axes of the slice: x: 2, y: 2, z: 4, core: 2. Of those that a mesh axis runs over, the one named last changes fastest.
Arguments:
- projected: bfloat16 [4, 4, 12, 128, 4096], P('section', 'seq', 'dp'), may hold values from -6 to 6
- dest_owner: int32 [4, 4, 12], P('section', 'seq', 'dp'), may hold values from 0 to 1, as said below
- slot_from: int32 [4, 2, 24], P('section', 'dp', 'seq'), may hold values from 0 to 5, as said below
- doc_starts: int32 [4, 2, 24], P('section', 'dp', 'seq'), may hold values from 0 to 1, as said below
- live_rows: int32 [4, 2, 24], P('section', 'dp', 'seq'), may hold values from 1 to 128, as said below
Outputs:
- attended: bfloat16 [4, 2, 3072, 2048], P('section', 'dp', 'seq')
The draws below stay inside these ranges and needn't reach their ends.
Inputs may be any that keep to these rules, and one draw needn't show every extreme that they name: `dest_owner`: in each column (t, s), every source device sends at most 3 blocks to one owner, some source sends exactly 3 blocks to some owner, and every owner receives exactly 6 blocks. Over all 4 columns (t, s) of one section t, source a sends at most 12 blocks to one owner, and some source sends exactly 12 to some owner. For owner o in column (t, s), slot_from[t, o, s * 6 + j] over j names each of the 6 numbers of the blocks that went to o in that column once. `doc_starts`: the first block of every pack begins a document; a document spans at most 8 blocks, and in every pack some document spans exactly 8. `live_rows`: 128 in every block but the last block of a document (the block before the next start, or the pack's last block).
All inputs are finite; a program needn't handle non-finite values.
Results may differ from the reference program's by a relative error of at most 0.0069.
Values may be sent and summed in bfloat16 or wider, within the bound.
A program may use at most 128 MiB of HBM per device.

```python
import jax
import jax.numpy as jnp
from jax import lax

HEADS = 8
KV_HEADS = 4
HEAD_DIM = 256
BLOCK = 128
DOC_MOST = 8
SRC_BLK = 6
SECTIONS = 4
SHARDS = 4
OWNERS = 2
SOURCES = 12
CAP = 3
PACK_BLK = 24
PACK_ROWS = 3072
WIDTH = 4096


def route_tables(key):
    section_keys = jax.random.split(jax.random.fold_in(key, 11), SECTIONS)

    def section_tables(section_key):
        subkeys = jax.random.split(section_key, 5)
        source_shift = jax.random.permutation(subkeys[0], OWNERS)
        owner_perm = jax.random.permutation(subkeys[1], OWNERS)
        offset_perm = jax.random.permutation(subkeys[2], OWNERS)
        shuffle_keys = jax.random.split(subkeys[3], SHARDS)
        order_keys = jax.random.split(subkeys[4], SHARDS)

        def column(shard_index, shuffle_key, order_key):
            offsets = offset_perm[(shard_index * SRC_BLK + jnp.arange(SRC_BLK, dtype=jnp.int32)) % OWNERS]

            def shuffle(subkey):
                return jax.random.permutation(subkey, SRC_BLK)
            shuffles = jax.vmap(shuffle)(jax.random.split(shuffle_key, OWNERS))
            owner_of = owner_perm[(source_shift[:, None] + offsets[shuffles]) % OWNERS].astype(jnp.int32)
            same_owner = owner_of[:, :, None] == owner_of[:, None, :]
            earlier = jnp.arange(SRC_BLK)[None, :] < jnp.arange(SRC_BLK)[:, None]
            ranking = jnp.sum(same_owner & earlier[None], axis=2).astype(jnp.int32)
            numbering = jnp.arange(OWNERS, dtype=jnp.int32)[:, None] * CAP + ranking
            flat_owner = owner_of.reshape(-1)
            tiebreak = jax.random.permutation(order_key, OWNERS * SRC_BLK).astype(jnp.int32)
            ordering = jnp.argsort(flat_owner * (OWNERS * SRC_BLK) + tiebreak, stable=True)
            slot_list = numbering.reshape(-1)[ordering].reshape(OWNERS, SRC_BLK)
            return (flat_owner, slot_list)
        return jax.vmap(column)(jnp.arange(SHARDS, dtype=jnp.int32), shuffle_keys, order_keys)
    owner_lists, slot_lists = jax.vmap(section_tables)(section_keys)
    owner_lists = owner_lists.reshape(SECTIONS, SHARDS, OWNERS * SRC_BLK)
    slot_lists = slot_lists.reshape(SECTIONS, SHARDS, OWNERS, SRC_BLK).transpose(0, 2, 1, 3).reshape(SECTIONS, OWNERS, PACK_BLK)
    return (owner_lists.astype(jnp.int32), slot_lists.astype(jnp.int32))


def document_tables(key):
    subkeys = jax.random.split(jax.random.fold_in(key, 23), 3)
    pack_count = SECTIONS * OWNERS
    lengths = jax.random.randint(subkeys[0], (pack_count, PACK_BLK), 1, DOC_MOST + 1)
    longest = jax.random.randint(subkeys[1], (pack_count, 1), 0, PACK_BLK // DOC_MOST)
    lengths = jnp.where(jnp.arange(PACK_BLK)[None, :] == longest, DOC_MOST, lengths)
    doc_ends = jnp.cumsum(lengths, axis=1)
    doc_begins = doc_ends - lengths
    block_ids = jnp.arange(PACK_BLK)
    start_flags = jnp.any(doc_begins[:, None, :] == block_ids[None, :, None], axis=2).astype(jnp.int32)
    closing = jnp.any(doc_ends[:, None, :] == (block_ids + 1)[None, :, None], axis=2) | (block_ids == PACK_BLK - 1)[None, :]
    tail_rows = jax.random.randint(subkeys[2], (pack_count, PACK_BLK), 1, BLOCK + 1)
    live_count = jnp.where(closing, tail_rows, BLOCK).astype(jnp.int32)
    return (start_flags.reshape(SECTIONS, OWNERS, PACK_BLK), live_count.reshape(SECTIONS, OWNERS, PACK_BLK))


def draw_projected(key, part):
    base_key = jax.random.fold_in(key, 37)
    half_width = HEAD_DIM // 2
    pair_index = jnp.arange(HEAD_DIM) % half_width
    slow_mask = (pair_index >= 3 * half_width // 4).astype(jnp.float32)
    direction = jnp.where(jax.random.bernoulli(jax.random.fold_in(key, 41), 0.5, (KV_HEADS, HEAD_DIM)), 1.0, -1.0)
    pattern = direction * slow_mask[None, :]
    group_size = HEADS // KV_HEADS

    def slab(number):
        slab_keys = jax.random.split(jax.random.fold_in(base_key, number), 4)
        noise_part = jax.random.normal(slab_keys[0], (SOURCES, BLOCK, WIDTH), jnp.float32)
        strength = jax.random.uniform(slab_keys[1], (SOURCES, BLOCK, 1), jnp.float32, 2.0, 3.5)
        picked = jax.random.bernoulli(slab_keys[2], 0.125, (SOURCES, BLOCK, 1))
        sign_flip = jnp.where(jax.random.bernoulli(slab_keys[3], 0.5, (SOURCES, BLOCK, KV_HEADS)), 1.0, -1.0)
        amount = jnp.where(picked, strength, 0.0) * sign_flip
        shared = amount[:, :, :, None] * pattern[None, None, :, :]
        query_add = jnp.broadcast_to(shared[:, :, :, None, :], (SOURCES, BLOCK, KV_HEADS, group_size, HEAD_DIM)).reshape(SOURCES, BLOCK, HEADS * HEAD_DIM)
        key_add = shared.reshape(SOURCES, BLOCK, KV_HEADS * HEAD_DIM)
        value_add = jnp.zeros((SOURCES, BLOCK, KV_HEADS * HEAD_DIM), jnp.float32)
        combined = noise_part + jnp.concatenate([query_add, key_add, value_add], axis=2)
        return jnp.clip(combined, -6.0, 6.0).astype(jnp.bfloat16)
    slabs = lax.map(slab, jnp.arange(SECTIONS * SHARDS, dtype=jnp.int32))
    return slabs.reshape(SECTIONS, SHARDS, SOURCES, BLOCK, WIDTH)


def draw_dest_owner(key, part):
    return route_tables(key)[0]


def draw_slot_from(key, part):
    return route_tables(key)[1]


def draw_doc_starts(key, part):
    return document_tables(key)[0]


def draw_live_rows(key, part):
    return document_tables(key)[1]


def setup_inputs(seed: int = 0) -> dict:
    keys = jax.random.split(jax.random.key(seed), 6)
    projected = draw_projected(jax.random.fold_in(keys[5], 71), 0)
    dest_owner = draw_dest_owner(jax.random.fold_in(keys[5], 71), 0)
    slot_from = draw_slot_from(jax.random.fold_in(keys[5], 71), 0)
    doc_starts = draw_doc_starts(jax.random.fold_in(keys[5], 71), 0)
    live_rows = draw_live_rows(jax.random.fold_in(keys[5], 71), 0)
    return dict(projected=projected, dest_owner=dest_owner, slot_from=slot_from, doc_starts=doc_starts, live_rows=live_rows)


score_cap = 50.0
rope_base = 10000.0


def rotate(columns, position, head_count):
    row_count = columns.shape[0]
    head_width = columns.shape[1] // head_count
    half_width = head_width // 2
    frequency = rope_base ** (-2.0 * jnp.arange(half_width, dtype=jnp.float32) / head_width)
    angles = position[:, None] * frequency[None, :]
    cosine = jnp.cos(angles)[:, None, :]
    sine_part = jnp.sin(angles)[:, None, :]
    split_heads = columns.astype(jnp.float32).reshape(row_count, head_count, head_width)
    first_half = split_heads[:, :, :half_width]
    second_half = split_heads[:, :, half_width:]
    turned = jnp.concatenate([first_half * cosine - second_half * sine_part, second_half * cosine + first_half * sine_part], axis=2)
    return turned.reshape(row_count, head_count * head_width).astype(jnp.bfloat16)


def source_choice(owner_list, slot_list):
    owner_grid = owner_list.reshape(OWNERS, SRC_BLK)
    same_owner = owner_grid[:, :, None] == owner_grid[:, None, :]
    earlier = jnp.arange(SRC_BLK)[None, :] < jnp.arange(SRC_BLK)[:, None]
    ranking = jnp.sum(same_owner & earlier[None], axis=2).astype(jnp.int32)
    located = owner_grid * (OWNERS * CAP) + jnp.arange(OWNERS, dtype=jnp.int32)[:, None] * CAP + ranking
    lookup = jnp.zeros((OWNERS * OWNERS * CAP,), jnp.int32).at[located.reshape(-1)].set(jnp.arange(OWNERS * SRC_BLK, dtype=jnp.int32))
    return lookup[jnp.arange(OWNERS, dtype=jnp.int32)[:, None] * (OWNERS * CAP) + slot_list]


def attend_pack(pack_rows, start_flags, live_count):
    query_width = HEADS * HEAD_DIM
    key_width = KV_HEADS * HEAD_DIM
    group_size = HEADS // KV_HEADS
    block_ids = jnp.arange(PACK_BLK, dtype=jnp.int32)
    doc_number = jnp.cumsum(start_flags).astype(jnp.int32) - 1
    doc_first = lax.cummax(jnp.where(start_flags == 1, block_ids, -1), axis=0)
    row_offset = jnp.arange(BLOCK, dtype=jnp.int32)
    position = ((block_ids - doc_first)[:, None] * BLOCK + row_offset[None, :]).reshape(-1).astype(jnp.float32)
    alive_rows = (row_offset[None, :] < live_count[:, None]).reshape(-1)
    doc_rows = jnp.repeat(doc_number, BLOCK)
    query_tag = jnp.where(alive_rows, doc_rows, -2)
    key_tag = jnp.where(alive_rows, doc_rows, -1)
    queries = rotate(pack_rows[:, :query_width], position, HEADS)
    key_rows = rotate(pack_rows[:, query_width:query_width + key_width], position, KV_HEADS)
    values = pack_rows[:, query_width + key_width:]
    margin = (DOC_MOST - 1) * BLOCK
    key_rows = jnp.concatenate([jnp.zeros((margin, key_width), key_rows.dtype), key_rows])
    values = jnp.concatenate([jnp.zeros((margin, key_width), values.dtype), values])
    key_tag = jnp.concatenate([jnp.full((margin,), -1, jnp.int32), key_tag])
    key_index = jnp.arange(PACK_ROWS + margin, dtype=jnp.int32) - margin
    query_index = jnp.arange(PACK_ROWS, dtype=jnp.int32)
    window = DOC_MOST * BLOCK

    def one_block(number):
        begin_row = number * BLOCK
        query_part = lax.dynamic_slice_in_dim(queries, begin_row, BLOCK, 0)
        key_part = lax.dynamic_slice_in_dim(key_rows, begin_row, window, 0)
        value_part = lax.dynamic_slice_in_dim(values, begin_row, window, 0)
        query_tags = lax.dynamic_slice_in_dim(query_tag, begin_row, BLOCK, 0)
        key_tags = lax.dynamic_slice_in_dim(key_tag, begin_row, window, 0)
        query_rows = lax.dynamic_slice_in_dim(query_index, begin_row, BLOCK, 0)
        key_rows_here = lax.dynamic_slice_in_dim(key_index, begin_row, window, 0)
        alive_here = lax.dynamic_slice_in_dim(alive_rows, begin_row, BLOCK, 0)
        grouped = lax.optimization_barrier(query_part).astype(jnp.float32).reshape(BLOCK, KV_HEADS, group_size, HEAD_DIM)
        keyed = lax.optimization_barrier(key_part).astype(jnp.float32).reshape(window, KV_HEADS, HEAD_DIM)
        scores = jnp.einsum("rhgd,khd->rhgk", grouped, keyed, precision=lax.Precision.HIGHEST) * HEAD_DIM ** -0.5
        capped = score_cap * jnp.tanh(scores / score_cap)
        allowed = (query_tags[:, None] == key_tags[None, :]) & (key_rows_here[None, :] <= query_rows[:, None])
        weight = jnp.where(allowed[:, None, None, :], jnp.exp(capped), 0.0)
        denominator = jnp.sum(weight, axis=3)
        rounded = lax.optimization_barrier(weight.astype(jnp.bfloat16)).astype(jnp.float32)
        valued = value_part.astype(jnp.float32).reshape(window, KV_HEADS, HEAD_DIM)
        numerator = jnp.einsum("rhgk,khd->rhgd", rounded, valued, precision=lax.Precision.HIGHEST)
        safe_total = jnp.where(alive_here[:, None, None], denominator, 1.0)
        averaged = jnp.where(alive_here[:, None, None, None], numerator / safe_total[:, :, :, None], 0.0)
        return averaged.reshape(BLOCK, query_width).astype(jnp.bfloat16)

    return lax.map(one_block, block_ids).reshape(PACK_ROWS, query_width)


def reference(projected, dest_owner, slot_from, doc_starts, live_rows):
    column_slots = slot_from.reshape(SECTIONS, OWNERS, SHARDS, SRC_BLK).transpose(0, 2, 1, 3)
    chosen = jax.vmap(jax.vmap(source_choice))(dest_owner, column_slots)

    def one_pack(number):
        section_index = number // OWNERS
        owner_index = number % OWNERS
        picks = chosen[section_index][:, owner_index]
        gathered = projected[section_index][jnp.arange(SHARDS, dtype=jnp.int32)[:, None], picks]
        pack_rows = gathered.reshape(PACK_ROWS, WIDTH)
        return attend_pack(pack_rows, doc_starts[section_index, owner_index], live_rows[section_index, owner_index])

    results = lax.map(one_pack, jnp.arange(SECTIONS * OWNERS, dtype=jnp.int32))
    results = results.reshape(SECTIONS, OWNERS, PACK_ROWS, HEADS * HEAD_DIM)
    return jnp.roll(results, 1, axis=0)
```

```python
import functools

import jax
import jax.numpy as jnp
from jax import lax
from jax.experimental import pallas as pl
from jax.experimental.pallas import tpu as pltpu
from jax.sharding import PartitionSpec as P

HEADS = 8
KV_HEADS = 4
HEAD_DIM = 256
DOC_MOST = 8
GROUP = HEADS // KV_HEADS

score_cap = 50.0
rope_base = 10000.0
log2_e = 1.4426950408889634


def shifted(block, axis, distance):
    count = lax.axis_size(axis)
    return lax.ppermute(block, axis, [(i, i + distance) for i in range(count - distance)])


def passed_along(block, axis, distance):
    count = lax.axis_size(axis)
    return lax.ppermute(block, axis, [((i - distance) % count, i) for i in range(count)])


def pick_kernel(flags_ref, source_ref, *out_refs):
    query_width = HEADS * HEAD_DIM
    key_width = KV_HEADS * HEAD_DIM
    wide = GROUP * HEAD_DIM
    for g in range(KV_HEADS):
        out_refs[2 * g][0] = source_ref[0, :, g * wide : (g + 1) * wide]
        begin = query_width + g * HEAD_DIM
        out_refs[2 * g + 1][0, :, :HEAD_DIM] = source_ref[0, :, begin : begin + HEAD_DIM]
        begin += key_width
        out_refs[2 * g + 1][0, :, HEAD_DIM:] = source_ref[0, :, begin : begin + HEAD_DIM]


def pick_blocks(flags, sources, capacity):
    blocks, rows, full_width = sources.shape
    wide = GROUP * HEAD_DIM

    def place(k, flags_ref):
        seen = jnp.int32(0)
        found = jnp.int32(0)
        for b in range(blocks):
            hit = flags_ref[b]
            found = jnp.where((hit == 1) & (seen == k), b, found)
            seen = seen + hit
        return (found, 0, 0)

    widths = [wide, 2 * HEAD_DIM] * KV_HEADS
    size = capacity * rows * full_width * 2
    return pl.pallas_call(
        pick_kernel,
        out_shape=[jax.ShapeDtypeStruct((capacity, rows, w), sources.dtype) for w in widths],
        grid_spec=pltpu.PrefetchScalarGridSpec(
            num_scalar_prefetch=1,
            grid=(capacity,),
            in_specs=[pl.BlockSpec((1, rows, full_width), place)],
            out_specs=[pl.BlockSpec((1, rows, w), lambda k, flags_ref: (k, 0, 0)) for w in widths],
        ),
        cost_estimate=pl.CostEstimate(flops=0, bytes_accessed=2 * size, transcendentals=0),
    )(flags, sources)


def attend_kernel(parts, blocks, extra, capacity, table_ref, *refs):
    q_refs = refs[:parts]
    own_refs = refs[parts : 2 * parts]
    prior_refs = refs[2 * parts : 3 * parts]
    extra_ref, cos_ref, sin_ref, out_ref, k_ref, v_ref, acc_ref, den_ref = refs[3 * parts :]
    rows = extra_ref.shape[1]
    half = HEAD_DIM // 2
    before = extra + blocks
    window = before + blocks
    pad = 1
    pos_at, first_at, live_at = window, 2 * window, 2 * window + blocks

    def turned(x, where):
        start = pl.multiple_of(where * rows, rows)
        c = cos_ref[pl.ds(start, rows), :]
        s = sin_ref[pl.ds(start, rows), :]
        x1 = x[:, :half].astype(jnp.float32)
        x2 = x[:, half:].astype(jnp.float32)
        return jnp.concatenate([x1 * c - x2 * s, x2 * c + x1 * s], axis=1).astype(jnp.bfloat16)

    def put(i, kv):
        begin = pl.multiple_of((i + pad) * rows, rows)
        k_ref[pl.ds(begin, rows), :] = turned(kv[:, :HEAD_DIM], table_ref[pos_at + i])
        v_ref[pl.ds(begin, rows), :] = kv[:, HEAD_DIM:]

    k_ref[pl.ds(0, rows), :] = jnp.zeros((rows, HEAD_DIM), jnp.bfloat16)
    v_ref[pl.ds(0, rows), :] = jnp.zeros((rows, HEAD_DIM), jnp.bfloat16)
    for i in range(extra):
        put(i, extra_ref[i])

    def chosen(part_refs, code, use):
        for n in range(parts):

            @pl.when((code >= n * capacity) & (code < (n + 1) * capacity))
            def _():
                use(part_refs[n][code - n * capacity])

    @pl.loop(extra, before)
    def _(i):
        chosen(prior_refs, table_ref[i], functools.partial(put, i))

    @pl.loop(before, window)
    def _(i):
        chosen(own_refs, table_ref[i], functools.partial(put, i))

    step = 2 * rows
    q_row = lax.broadcasted_iota(jnp.int32, (rows, step), 0)
    k_col = lax.broadcasted_iota(jnp.int32, (rows, step), 1)
    gap = k_col - q_row

    @pl.loop(0, blocks)
    def _(j):
        here = table_ref[pos_at + before + j]

        def run(q):
            q2 = jnp.concatenate(
                [turned(q[:, h * HEAD_DIM : (h + 1) * HEAD_DIM], here) for h in range(GROUP)], axis=0
            )
            acc_ref[...] = jnp.zeros_like(acc_ref)
            den_ref[...] = jnp.zeros_like(den_ref)
            first = table_ref[first_at + j]
            last = before + j

            @pl.loop(0, (last - first) // 2 + 1)
            def _(n):
                low = last - 1 - 2 * n
                begin = pl.multiple_of((low + pad) * rows, rows)
                k = k_ref[pl.ds(begin, step), :]
                v = v_ref[pl.ds(begin, step), :]
                s = lax.dot_general(
                    q2, k, (((1,), (1,)), ((), ())), preferred_element_type=jnp.float32
                )
                t = jnp.tanh(s * (HEAD_DIM**-0.5 / score_cap))
                w = jnp.exp2(t * (score_cap * log2_e))
                seen = (gap <= (last - low) * rows) & (k_col >= (first - low) * rows)
                seen = jnp.concatenate([seen] * GROUP, axis=0)
                w = jnp.where(seen, w, 0.0)
                den_ref[...] += w[:, :rows] + w[:, rows:]
                acc_ref[...] += jnp.dot(
                    w.astype(jnp.bfloat16), v, preferred_element_type=jnp.float32
                )

            total = jnp.sum(den_ref[...], axis=1, keepdims=True)
            mean = acc_ref[...] / total
            alive = (
                lax.broadcasted_iota(jnp.int32, (rows, HEAD_DIM), 0) < table_ref[live_at + j]
            )
            begin = pl.multiple_of(j * rows, rows)
            for h in range(GROUP):
                out_ref[pl.ds(begin, rows), h * HEAD_DIM : (h + 1) * HEAD_DIM] = jnp.where(
                    alive, mean[h * rows : (h + 1) * rows], 0.0
                ).astype(jnp.bfloat16)

        chosen(q_refs, table_ref[before + j], run)


def attend(table, queries, own, prior, beyond, cosine, sine):
    parts = len(queries)
    capacity, rows, wide = queries[0].shape
    blocks = parts * capacity
    extra = beyond.shape[0]
    window = extra + 2 * blocks
    spec = pl.BlockSpec(memory_space=pltpu.VMEM)
    pairs = blocks * (DOC_MOST // 2 + 1)
    return pl.pallas_call(
        functools.partial(attend_kernel, parts, blocks, extra, capacity),
        out_shape=jax.ShapeDtypeStruct((blocks * rows, wide), jnp.bfloat16),
        in_specs=[pl.BlockSpec(memory_space=pltpu.SMEM)] + [spec] * (3 * parts + 3),
        out_specs=spec,
        scratch_shapes=[
            pltpu.VMEM(((window + 1) * rows, HEAD_DIM), jnp.bfloat16),
            pltpu.VMEM(((window + 1) * rows, HEAD_DIM), jnp.bfloat16),
            pltpu.VMEM((GROUP * rows, HEAD_DIM), jnp.float32),
            pltpu.VMEM((GROUP * rows, rows), jnp.float32),
        ],
        cost_estimate=pl.CostEstimate(
            flops=pairs * 8 * GROUP * rows * rows * HEAD_DIM,
            bytes_accessed=4 * blocks * rows * wide * 2,
            transcendentals=pairs * 4 * GROUP * rows * rows,
        ),
    )(table, *queries, *own, *prior, beyond, cosine, sine)


def shards(projected, dest_owner, slot_from, doc_starts, live_rows):
    sources = projected[0, 0]
    blocks, rows, full_width = sources.shape
    dp_count = lax.axis_size("dp")
    capacity = (blocks + dp_count - 1) // dp_count
    owners = dest_owner[0, 0]
    numbers = slot_from[0, 0]
    starts = doc_starts[0, 0]
    me = lax.axis_index("dp")
    extra = DOC_MOST - 1 - blocks

    if dp_count == 2:
        mine = (owners == me).astype(jnp.int32)
        away = pick_blocks(1 - mine, sources, capacity)
        home = pick_blocks(mine, sources, capacity)
        arrived = [passed_along(a, "dp", 1) for a in away]
        heads = [
            ((home[2 * g], arrived[2 * g]), (home[2 * g + 1], arrived[2 * g + 1]))
            for g in range(KV_HEADS)
        ]
        codes = numbers % capacity + jnp.where(numbers // capacity == me, 0, capacity)
    else:
        earlier = jnp.tril(jnp.ones((blocks, blocks), jnp.int32), -1)
        rank = jnp.sum((owners[:, None] == owners[None, :]) * earlier, axis=1)
        target = owners * capacity + rank
        hits = target[None, :] == jnp.arange(dp_count * capacity)[:, None]
        order = jnp.sum(jnp.where(hits, jnp.arange(blocks)[None, :], 0), axis=1)
        got = lax.all_to_all(
            jnp.take(sources, order, axis=0), "dp", split_axis=0, concat_axis=0, tiled=True
        )
        packed = jnp.take(got, numbers, axis=0)
        everything = pick_blocks(jnp.ones((blocks,), jnp.int32), packed, blocks)
        heads = [((everything[2 * g],), (everything[2 * g + 1],)) for g in range(KV_HEADS)]
        codes = jnp.arange(blocks, dtype=jnp.int32)

    both = jnp.concatenate([codes, starts]).astype(jnp.int32)
    below = shifted(both, "seq", 1)
    beneath = shifted(starts, "seq", 2)
    flags = jnp.concatenate([beneath[blocks - extra :], below[blocks:], starts])
    window = extra + 2 * blocks
    ids = jnp.arange(window, dtype=jnp.int32)
    before = extra + blocks
    opened = (flags[None, :] == 1) & (ids[None, :] <= ids[:, None])
    first = jnp.max(jnp.where(opened, ids[None, :], 0), axis=1)
    at_start = first[before]
    position = jnp.where(ids < before, ids - at_start, ids - first)
    position = jnp.clip(position, 0, DOC_MOST - 1)
    table = jnp.concatenate(
        [
            jnp.zeros((extra,), jnp.int32),
            below[:blocks],
            codes.astype(jnp.int32),
            position,
            first[before:],
            live_rows[0, 0],
        ]
    )

    half = HEAD_DIM // 2
    frequency = rope_base ** (-2.0 * jnp.arange(half, dtype=jnp.float32) / HEAD_DIM)
    angles = jnp.arange(DOC_MOST * rows, dtype=jnp.float32)[:, None] * frequency[None, :]
    cosine, sine = jnp.cos(angles), jnp.sin(angles)

    def tail(kv):
        picked = []
        for e in range(extra):
            code = codes[blocks - extra + e]
            size = kv[0].shape[0]
            best = lax.dynamic_slice_in_dim(kv[0], jnp.clip(code, 0, size - 1), 1, 0)
            for n in range(1, len(kv)):
                other = lax.dynamic_slice_in_dim(
                    kv[n], jnp.clip(code - n * size, 0, size - 1), 1, 0
                )
                best = jnp.where(code >= n * size, other, best)
            picked.append(best)
        return jnp.concatenate(picked)

    handed = []
    for queries, kv in heads:
        prior = tuple(shifted(part, "seq", 1) for part in kv)
        beyond = shifted(tail(kv), "seq", 2)
        out = attend(table, queries, kv, prior, beyond, cosine, sine)
        handed.append(passed_along(out, "section", 1))
    return jnp.concatenate(handed, axis=1)[None, None]


def solution(mesh):
    placed = (
        P("section", "seq", "dp", None, None),
        P("section", "seq", "dp"),
        P("section", "dp", "seq"),
        P("section", "dp", "seq"),
        P("section", "dp", "seq"),
    )
    return jax.shard_map(
        shards,
        mesh=mesh,
        in_specs=placed,
        out_specs=P("section", "dp", "seq", None),
        check_vma=False,
    )
```

```python
import functools

import jax
import jax.numpy as jnp
from jax import lax
from jax.experimental import pallas as pl
from jax.experimental.pallas import tpu as pltpu
from jax.sharding import PartitionSpec as P

HEADS = 8
KV_HEADS = 4
HEAD_DIM = 256
DOC_MOST = 8
GROUP = HEADS // KV_HEADS

score_cap = 50.0
rope_base = 10000.0
log2_e = 1.4426950408889634


def shifted(block, axis, distance):
    count = lax.axis_size(axis)
    return lax.ppermute(block, axis, [(i, i + distance) for i in range(count - distance)])


def passed_along(block, axis, distance):
    count = lax.axis_size(axis)
    return lax.ppermute(block, axis, [((i - distance) % count, i) for i in range(count)])


def pick_queries(flags_ref, source_ref, *out_refs):
    wide = GROUP * HEAD_DIM
    for g in range(KV_HEADS):
        out_refs[g][0] = source_ref[0, :, g * wide : (g + 1) * wide]


def pick_keys(flags_ref, source_ref, *out_refs):
    key_width = KV_HEADS * HEAD_DIM
    for g in range(KV_HEADS):
        begin = g * HEAD_DIM
        out_refs[g][0, :, :HEAD_DIM] = source_ref[0, :, begin : begin + HEAD_DIM]
        begin += key_width
        out_refs[g][0, :, HEAD_DIM:] = source_ref[0, :, begin : begin + HEAD_DIM]


def pick_blocks(kernel, flags, sources, capacity):
    blocks, rows, full_width = sources.shape
    column = 0 if kernel is pick_queries else 1

    def place(k, flags_ref):
        seen = jnp.int32(0)
        found = jnp.int32(0)
        for b in range(blocks):
            hit = flags_ref[b]
            found = jnp.where((hit == 1) & (seen == k), b, found)
            seen = seen + hit
        return (found, 0, column)

    width = full_width // 2
    each = width // KV_HEADS
    return pl.pallas_call(
        kernel,
        out_shape=[jax.ShapeDtypeStruct((capacity, rows, each), sources.dtype)] * KV_HEADS,
        grid_spec=pltpu.PrefetchScalarGridSpec(
            num_scalar_prefetch=1,
            grid=(capacity,),
            in_specs=[pl.BlockSpec((1, rows, width), place)],
            out_specs=[pl.BlockSpec((1, rows, each), lambda k, flags_ref: (k, 0, 0))] * KV_HEADS,
        ),
        cost_estimate=pl.CostEstimate(
            flops=0, bytes_accessed=2 * capacity * rows * width * 2, transcendentals=0
        ),
    )(flags, sources)


def attend_kernel(parts, blocks, extra, capacity, table_ref, *refs):
    q_refs = refs[:parts]
    own_refs = refs[parts : 2 * parts]
    prior_refs = refs[2 * parts : 3 * parts]
    extra_ref, cos_ref, sin_ref, out_ref, k_ref, v_ref, acc_ref, den_ref = refs[3 * parts :]
    rows = extra_ref.shape[1]
    half = HEAD_DIM // 2
    before = extra + blocks
    window = before + blocks
    pad = 1
    pos_at, first_at, live_at = window, 2 * window, 2 * window + blocks

    def turned(x, where):
        start = pl.multiple_of(where * rows, rows)
        c = cos_ref[pl.ds(start, rows), :]
        s = sin_ref[pl.ds(start, rows), :]
        x1 = x[:, :half].astype(jnp.float32)
        x2 = x[:, half:].astype(jnp.float32)
        return jnp.concatenate([x1 * c - x2 * s, x2 * c + x1 * s], axis=1).astype(jnp.bfloat16)

    def put(i, kv):
        begin = pl.multiple_of((i + pad) * rows, rows)
        k_ref[pl.ds(begin, rows), :] = turned(kv[:, :HEAD_DIM], table_ref[pos_at + i])
        v_ref[pl.ds(begin, rows), :] = kv[:, HEAD_DIM:]

    k_ref[pl.ds(0, rows), :] = jnp.zeros((rows, HEAD_DIM), jnp.bfloat16)
    v_ref[pl.ds(0, rows), :] = jnp.zeros((rows, HEAD_DIM), jnp.bfloat16)
    for i in range(extra):
        put(i, extra_ref[i])

    def chosen(part_refs, code, use):
        for n in range(parts):

            @pl.when((code >= n * capacity) & (code < (n + 1) * capacity))
            def _():
                use(part_refs[n][code - n * capacity])

    @pl.loop(extra, before)
    def _(i):
        chosen(prior_refs, table_ref[i], functools.partial(put, i))

    @pl.loop(before, window)
    def _(i):
        chosen(own_refs, table_ref[i], functools.partial(put, i))

    step = 2 * rows
    q_row = lax.broadcasted_iota(jnp.int32, (rows, step), 0)
    k_col = lax.broadcasted_iota(jnp.int32, (rows, step), 1)
    gap = k_col - q_row

    @pl.loop(0, blocks)
    def _(j):
        here = table_ref[pos_at + before + j]

        def run(q):
            q2 = jnp.concatenate(
                [turned(q[:, h * HEAD_DIM : (h + 1) * HEAD_DIM], here) for h in range(GROUP)], axis=0
            )
            acc_ref[...] = jnp.zeros_like(acc_ref)
            den_ref[...] = jnp.zeros_like(den_ref)
            first = table_ref[first_at + j]
            last = before + j

            @pl.loop(0, (last - first) // 2 + 1)
            def _(n):
                low = last - 1 - 2 * n
                begin = pl.multiple_of((low + pad) * rows, rows)
                k = k_ref[pl.ds(begin, step), :]
                v = v_ref[pl.ds(begin, step), :]
                s = lax.dot_general(
                    q2, k, (((1,), (1,)), ((), ())), preferred_element_type=jnp.float32
                )
                t = jnp.tanh(s * (HEAD_DIM**-0.5 / score_cap))
                w = jnp.exp2(t * (score_cap * log2_e))
                seen = (gap <= (last - low) * rows) & (k_col >= (first - low) * rows)
                seen = jnp.concatenate([seen] * GROUP, axis=0)
                w = jnp.where(seen, w, 0.0)
                den_ref[...] += w[:, :rows] + w[:, rows:]
                acc_ref[...] += jnp.dot(
                    w.astype(jnp.bfloat16), v, preferred_element_type=jnp.float32
                )

            total = jnp.sum(den_ref[...], axis=1, keepdims=True)
            mean = acc_ref[...] / total
            alive = (
                lax.broadcasted_iota(jnp.int32, (rows, HEAD_DIM), 0) < table_ref[live_at + j]
            )
            begin = pl.multiple_of(j * rows, rows)
            for h in range(GROUP):
                out_ref[pl.ds(begin, rows), h * HEAD_DIM : (h + 1) * HEAD_DIM] = jnp.where(
                    alive, mean[h * rows : (h + 1) * rows], 0.0
                ).astype(jnp.bfloat16)

        chosen(q_refs, table_ref[before + j], run)


def attend(table, queries, own, prior, beyond, cosine, sine):
    parts = len(queries)
    capacity, rows, wide = queries[0].shape
    blocks = parts * capacity
    extra = beyond.shape[0]
    window = extra + 2 * blocks
    spec = pl.BlockSpec(memory_space=pltpu.VMEM)
    pairs = blocks * (DOC_MOST // 2 + 1)
    return pl.pallas_call(
        functools.partial(attend_kernel, parts, blocks, extra, capacity),
        out_shape=jax.ShapeDtypeStruct((blocks * rows, wide), jnp.bfloat16),
        in_specs=[pl.BlockSpec(memory_space=pltpu.SMEM)] + [spec] * (3 * parts + 3),
        out_specs=spec,
        scratch_shapes=[
            pltpu.VMEM(((window + 1) * rows, HEAD_DIM), jnp.bfloat16),
            pltpu.VMEM(((window + 1) * rows, HEAD_DIM), jnp.bfloat16),
            pltpu.VMEM((GROUP * rows, HEAD_DIM), jnp.float32),
            pltpu.VMEM((GROUP * rows, rows), jnp.float32),
        ],
        cost_estimate=pl.CostEstimate(
            flops=pairs * 8 * GROUP * rows * rows * HEAD_DIM,
            bytes_accessed=4 * blocks * rows * wide * 2,
            transcendentals=pairs * 4 * GROUP * rows * rows,
        ),
    )(table, *queries, *own, *prior, beyond, cosine, sine)


def shards(projected, dest_owner, slot_from, doc_starts, live_rows):
    sources = projected[0, 0]
    blocks, rows, full_width = sources.shape
    dp_count = lax.axis_size("dp")
    capacity = (blocks + dp_count - 1) // dp_count
    owners = dest_owner[0, 0]
    numbers = slot_from[0, 0]
    starts = doc_starts[0, 0]
    me = lax.axis_index("dp")
    extra = DOC_MOST - 1 - blocks

    if dp_count == 2:
        mine = (owners == me).astype(jnp.int32)
        home_kv = list(pick_blocks(pick_keys, mine, sources, capacity))
        theirs, mine, home_kv[0] = lax.optimization_barrier((1 - mine, mine, home_kv[0]))
        away_kv = pick_blocks(pick_keys, theirs, sources, capacity)
        away_q = pick_blocks(pick_queries, theirs, sources, capacity)
        home_q = pick_blocks(pick_queries, mine, sources, capacity)
        heads = []
        for g in range(KV_HEADS):
            kv = passed_along(away_kv[g], "dp", 1)
            kv, query = lax.optimization_barrier((kv, away_q[g]))
            query = passed_along(query, "dp", 1)
            heads.append(((home_q[g], query), (home_kv[g], kv)))
        codes = numbers % capacity + jnp.where(numbers // capacity == me, 0, capacity)
    else:
        earlier = jnp.tril(jnp.ones((blocks, blocks), jnp.int32), -1)
        rank = jnp.sum((owners[:, None] == owners[None, :]) * earlier, axis=1)
        target = owners * capacity + rank
        hits = target[None, :] == jnp.arange(dp_count * capacity)[:, None]
        order = jnp.sum(jnp.where(hits, jnp.arange(blocks)[None, :], 0), axis=1)
        got = lax.all_to_all(
            jnp.take(sources, order, axis=0), "dp", split_axis=0, concat_axis=0, tiled=True
        )
        packed = jnp.take(got, numbers, axis=0)
        every = jnp.ones((blocks,), jnp.int32)
        queries = pick_blocks(pick_queries, every, packed, blocks)
        keys = pick_blocks(pick_keys, every, packed, blocks)
        heads = [((queries[g],), (keys[g],)) for g in range(KV_HEADS)]
        codes = jnp.arange(blocks, dtype=jnp.int32)

    both = jnp.concatenate([codes, starts]).astype(jnp.int32)
    below = shifted(both, "seq", 1)
    beneath = shifted(starts, "seq", 2)
    flags = jnp.concatenate([beneath[blocks - extra :], below[blocks:], starts])
    window = extra + 2 * blocks
    ids = jnp.arange(window, dtype=jnp.int32)
    before = extra + blocks
    opened = (flags[None, :] == 1) & (ids[None, :] <= ids[:, None])
    first = jnp.max(jnp.where(opened, ids[None, :], 0), axis=1)
    at_start = first[before]
    position = jnp.where(ids < before, ids - at_start, ids - first)
    position = jnp.clip(position, 0, DOC_MOST - 1)
    table = jnp.concatenate(
        [
            jnp.zeros((extra,), jnp.int32),
            below[:blocks],
            codes.astype(jnp.int32),
            position,
            first[before:],
            live_rows[0, 0],
        ]
    )

    half = HEAD_DIM // 2
    frequency = rope_base ** (-2.0 * jnp.arange(half, dtype=jnp.float32) / HEAD_DIM)
    angles = jnp.arange(DOC_MOST * rows, dtype=jnp.float32)[:, None] * frequency[None, :]
    cosine, sine = jnp.cos(angles), jnp.sin(angles)

    def tail(kv):
        picked = []
        for e in range(extra):
            code = codes[blocks - extra + e]
            size = kv[0].shape[0]
            best = lax.dynamic_slice_in_dim(kv[0], jnp.clip(code, 0, size - 1), 1, 0)
            for n in range(1, len(kv)):
                other = lax.dynamic_slice_in_dim(
                    kv[n], jnp.clip(code - n * size, 0, size - 1), 1, 0
                )
                best = jnp.where(code >= n * size, other, best)
            picked.append(best)
        return jnp.concatenate(picked)

    handed = []
    for queries, kv in heads:
        prior = tuple(shifted(part, "seq", 1) for part in kv)
        beyond = shifted(tail(kv), "seq", 2)
        out = attend(table, queries, kv, prior, beyond, cosine, sine)
        handed.append(passed_along(out, "section", 1))
    return jnp.concatenate(handed, axis=1)[None, None]


def solution(mesh):
    placed = (
        P("section", "seq", "dp", None, None),
        P("section", "seq", "dp"),
        P("section", "dp", "seq"),
        P("section", "dp", "seq"),
        P("section", "dp", "seq"),
    )
    return jax.shard_map(
        shards,
        mesh=mesh,
        in_specs=placed,
        out_specs=P("section", "dp", "seq", None),
        check_vma=False,
    )
```

```python
import functools

import jax
import jax.numpy as jnp
from jax import lax
from jax.experimental import pallas as pl
from jax.experimental.pallas import tpu as pltpu
from jax.sharding import PartitionSpec as P

HEADS = 8
KV_HEADS = 4
HEAD_DIM = 256
DOC_MOST = 8
GROUP = HEADS // KV_HEADS

score_cap = 50.0
rope_base = 10000.0
log2_e = 1.4426950408889634


def shifted(block, axis, distance):
    count = lax.axis_size(axis)
    return lax.ppermute(block, axis, [(i, i + distance) for i in range(count - distance)])


def passed_along(block, axis, distance):
    count = lax.axis_size(axis)
    return lax.ppermute(block, axis, [((i - distance) % count, i) for i in range(count)])


def pick_queries(flags_ref, source_ref, *out_refs):
    wide = GROUP * HEAD_DIM
    for g in range(KV_HEADS):
        out_refs[g][0] = source_ref[0, :, g * wide : (g + 1) * wide]


def pick_keys(flags_ref, source_ref, *out_refs):
    key_width = KV_HEADS * HEAD_DIM
    for g in range(KV_HEADS):
        begin = g * HEAD_DIM
        out_refs[g][0, :, :HEAD_DIM] = source_ref[0, :, begin : begin + HEAD_DIM]
        begin += key_width
        out_refs[g][0, :, HEAD_DIM:] = source_ref[0, :, begin : begin + HEAD_DIM]


def pick_blocks(kernel, flags, sources, capacity):
    blocks, rows, full_width = sources.shape
    column = 0 if kernel is pick_queries else 1

    def place(k, flags_ref):
        seen = jnp.int32(0)
        found = jnp.int32(0)
        for b in range(blocks):
            hit = flags_ref[b]
            found = jnp.where((hit == 1) & (seen == k), b, found)
            seen = seen + hit
        return (found, 0, column)

    width = full_width // 2
    each = width // KV_HEADS
    return pl.pallas_call(
        kernel,
        out_shape=[jax.ShapeDtypeStruct((capacity, rows, each), sources.dtype)] * KV_HEADS,
        grid_spec=pltpu.PrefetchScalarGridSpec(
            num_scalar_prefetch=1,
            grid=(capacity,),
            in_specs=[pl.BlockSpec((1, rows, width), place)],
            out_specs=[pl.BlockSpec((1, rows, each), lambda k, flags_ref: (k, 0, 0))] * KV_HEADS,
        ),
        cost_estimate=pl.CostEstimate(
            flops=0, bytes_accessed=2 * capacity * rows * width * 2, transcendentals=0
        ),
    )(flags, sources)


def attend_kernel(parts, blocks, extra, capacity, table_ref, *refs):
    q_refs = refs[:parts]
    own_refs = refs[parts : 2 * parts]
    prior_refs = refs[2 * parts : 3 * parts]
    extra_ref, cos_ref, sin_ref, out_ref, k_ref, v_ref, acc_ref, den_ref = refs[3 * parts :]
    rows = extra_ref.shape[1]
    half = HEAD_DIM // 2
    before = extra + blocks
    window = before + blocks
    pad = 1
    pos_at, first_at, live_at = window, 2 * window, 2 * window + blocks

    def turned(x, where):
        start = pl.multiple_of(where * rows, rows)
        c = cos_ref[pl.ds(start, rows), :]
        s = sin_ref[pl.ds(start, rows), :]
        x1 = x[:, :half].astype(jnp.float32)
        x2 = x[:, half:].astype(jnp.float32)
        return jnp.concatenate([x1 * c - x2 * s, x2 * c + x1 * s], axis=1).astype(jnp.bfloat16)

    def put(i, kv):
        begin = pl.multiple_of((i + pad) * rows, rows)
        k_ref[pl.ds(begin, rows), :] = turned(kv[:, :HEAD_DIM], table_ref[pos_at + i])
        v_ref[pl.ds(begin, rows), :] = kv[:, HEAD_DIM:]

    k_ref[pl.ds(0, rows), :] = jnp.zeros((rows, HEAD_DIM), jnp.bfloat16)
    v_ref[pl.ds(0, rows), :] = jnp.zeros((rows, HEAD_DIM), jnp.bfloat16)
    for i in range(extra):
        put(i, extra_ref[i])

    def chosen(part_refs, code, use):
        for n in range(parts):

            @pl.when((code >= n * capacity) & (code < (n + 1) * capacity))
            def _():
                use(part_refs[n][code - n * capacity])

    @pl.loop(extra, before)
    def _(i):
        chosen(prior_refs, table_ref[i], functools.partial(put, i))

    @pl.loop(before, window)
    def _(i):
        chosen(own_refs, table_ref[i], functools.partial(put, i))

    step = 2 * rows
    q_row = lax.broadcasted_iota(jnp.int32, (rows, step), 0)
    k_col = lax.broadcasted_iota(jnp.int32, (rows, step), 1)
    gap = k_col - q_row

    @pl.loop(0, blocks)
    def _(j):
        here = table_ref[pos_at + before + j]

        def run(q):
            q2 = jnp.concatenate(
                [turned(q[:, h * HEAD_DIM : (h + 1) * HEAD_DIM], here) for h in range(GROUP)], axis=0
            )
            acc_ref[...] = jnp.zeros_like(acc_ref)
            den_ref[...] = jnp.zeros_like(den_ref)
            first = table_ref[first_at + j]
            last = before + j

            @pl.loop(0, (last - first) // 2 + 1)
            def _(n):
                low = last - 1 - 2 * n
                begin = pl.multiple_of((low + pad) * rows, rows)
                k = k_ref[pl.ds(begin, step), :]
                v = v_ref[pl.ds(begin, step), :]
                s = lax.dot_general(
                    q2, k, (((1,), (1,)), ((), ())), preferred_element_type=jnp.float32
                )
                t = jnp.tanh(s * (HEAD_DIM**-0.5 / score_cap))
                w = jnp.exp2(t * (score_cap * log2_e))
                seen = (gap <= (last - low) * rows) & (k_col >= (first - low) * rows)
                seen = jnp.concatenate([seen] * GROUP, axis=0)
                w = jnp.where(seen, w, 0.0)
                den_ref[...] += w[:, :rows] + w[:, rows:]
                acc_ref[...] += jnp.dot(
                    w.astype(jnp.bfloat16), v, preferred_element_type=jnp.float32
                )

            total = jnp.sum(den_ref[...], axis=1, keepdims=True)
            mean = acc_ref[...] / total
            alive = (
                lax.broadcasted_iota(jnp.int32, (rows, HEAD_DIM), 0) < table_ref[live_at + j]
            )
            begin = pl.multiple_of(j * rows, rows)
            for h in range(GROUP):
                out_ref[pl.ds(begin, rows), h * HEAD_DIM : (h + 1) * HEAD_DIM] = jnp.where(
                    alive, mean[h * rows : (h + 1) * rows], 0.0
                ).astype(jnp.bfloat16)

        chosen(q_refs, table_ref[before + j], run)


def attend(table, queries, own, prior, beyond, cosine, sine):
    parts = len(queries)
    capacity, rows, wide = queries[0].shape
    blocks = parts * capacity
    extra = beyond.shape[0]
    window = extra + 2 * blocks
    spec = pl.BlockSpec(memory_space=pltpu.VMEM)
    pairs = blocks * (DOC_MOST // 2 + 1)
    return pl.pallas_call(
        functools.partial(attend_kernel, parts, blocks, extra, capacity),
        out_shape=jax.ShapeDtypeStruct((blocks * rows, wide), jnp.bfloat16),
        in_specs=[pl.BlockSpec(memory_space=pltpu.SMEM)] + [spec] * (3 * parts + 3),
        out_specs=spec,
        scratch_shapes=[
            pltpu.VMEM(((window + 1) * rows, HEAD_DIM), jnp.bfloat16),
            pltpu.VMEM(((window + 1) * rows, HEAD_DIM), jnp.bfloat16),
            pltpu.VMEM((GROUP * rows, HEAD_DIM), jnp.float32),
            pltpu.VMEM((GROUP * rows, rows), jnp.float32),
        ],
        cost_estimate=pl.CostEstimate(
            flops=pairs * 8 * GROUP * rows * rows * HEAD_DIM,
            bytes_accessed=4 * blocks * rows * wide * 2,
            transcendentals=pairs * 4 * GROUP * rows * rows,
        ),
    )(table, *queries, *own, *prior, beyond, cosine, sine)


def shards(projected, dest_owner, slot_from, doc_starts, live_rows):
    sources = projected[0, 0]
    blocks, rows, full_width = sources.shape
    dp_count = lax.axis_size("dp")
    capacity = (blocks + dp_count - 1) // dp_count
    owners = dest_owner[0, 0]
    numbers = slot_from[0, 0]
    starts = doc_starts[0, 0]
    me = lax.axis_index("dp")
    extra = DOC_MOST - 1 - blocks

    if dp_count == 2:
        mine = (owners == me).astype(jnp.int32)
        home_kv = list(pick_blocks(pick_keys, mine, sources, capacity))
        theirs, mine, home_kv[0] = lax.optimization_barrier((1 - mine, mine, home_kv[0]))
        away_kv = pick_blocks(pick_keys, theirs, sources, capacity)
        away_q = pick_blocks(pick_queries, theirs, sources, capacity)
        home_q = pick_blocks(pick_queries, mine, sources, capacity)
        heads = []
        for g in range(KV_HEADS):
            kv = passed_along(away_kv[g], "dp", 1)
            kv, query = lax.optimization_barrier((kv, away_q[g]))
            query = passed_along(query, "dp", 1)
            heads.append(((home_q[g], query), (home_kv[g], kv)))
        codes = numbers % capacity + jnp.where(numbers // capacity == me, 0, capacity)
    else:
        earlier = jnp.tril(jnp.ones((blocks, blocks), jnp.int32), -1)
        rank = jnp.sum((owners[:, None] == owners[None, :]) * earlier, axis=1)
        target = owners * capacity + rank
        hits = target[None, :] == jnp.arange(dp_count * capacity)[:, None]
        order = jnp.sum(jnp.where(hits, jnp.arange(blocks)[None, :], 0), axis=1)
        got = lax.all_to_all(
            jnp.take(sources, order, axis=0), "dp", split_axis=0, concat_axis=0, tiled=True
        )
        packed = jnp.take(got, numbers, axis=0)
        every = jnp.ones((blocks,), jnp.int32)
        away_kv = [every]
        queries = pick_blocks(pick_queries, every, packed, blocks)
        keys = pick_blocks(pick_keys, every, packed, blocks)
        heads = [((queries[g],), (keys[g],)) for g in range(KV_HEADS)]
        codes = jnp.arange(blocks, dtype=jnp.int32)

    codes, starts, _ = lax.optimization_barrier((codes, starts, away_kv[0]))
    both = jnp.concatenate([codes, starts]).astype(jnp.int32)
    below = shifted(both, "seq", 1)
    beneath = shifted(starts, "seq", 2)
    flags = jnp.concatenate([beneath[blocks - extra :], below[blocks:], starts])
    window = extra + 2 * blocks
    ids = jnp.arange(window, dtype=jnp.int32)
    before = extra + blocks
    opened = (flags[None, :] == 1) & (ids[None, :] <= ids[:, None])
    first = jnp.max(jnp.where(opened, ids[None, :], 0), axis=1)
    at_start = first[before]
    position = jnp.where(ids < before, ids - at_start, ids - first)
    position = jnp.clip(position, 0, DOC_MOST - 1)
    table = jnp.concatenate(
        [
            jnp.zeros((extra,), jnp.int32),
            below[:blocks],
            codes.astype(jnp.int32),
            position,
            first[before:],
            live_rows[0, 0],
        ]
    )

    half = HEAD_DIM // 2
    frequency = rope_base ** (-2.0 * jnp.arange(half, dtype=jnp.float32) / HEAD_DIM)
    angles = jnp.arange(DOC_MOST * rows, dtype=jnp.float32)[:, None] * frequency[None, :]
    cosine, sine = jnp.cos(angles), jnp.sin(angles)

    def tail(kv, codes):
        picked = []
        for e in range(extra):
            code = codes[blocks - extra + e]
            size = kv[0].shape[0]
            best = lax.dynamic_slice_in_dim(kv[0], jnp.clip(code, 0, size - 1), 1, 0)
            for n in range(1, len(kv)):
                other = lax.dynamic_slice_in_dim(
                    kv[n], jnp.clip(code - n * size, 0, size - 1), 1, 0
                )
                best = jnp.where(code >= n * size, other, best)
            picked.append(best)
        return jnp.concatenate(picked)

    def after(block, *earlier):
        return lax.optimization_barrier((block, *earlier))[0]

    priors = []
    for g, (queries, kv) in enumerate(heads):
        kv = list(kv)
        if len(kv) == 2:
            if g == 2:
                kv[0] = after(kv[0], heads[0][1][1])
            if g == 3:
                kv[0] = after(kv[0], priors[0][1])
            if g >= 2:
                kv[1] = after(kv[1], priors[g - 2][1])
        priors.append(tuple(shifted(part, "seq", 1) for part in kv))
    handed = []
    for g, (queries, kv) in enumerate(heads):
        beyond = shifted(tail(priors[g], below[:blocks]), "seq", 1)
        out = attend(table, queries, kv, priors[g], beyond, cosine, sine)
        handed.append(passed_along(out, "section", 1))
    return jnp.concatenate(handed, axis=1)[None, None]


def solution(mesh):
    placed = (
        P("section", "seq", "dp", None, None),
        P("section", "seq", "dp"),
        P("section", "dp", "seq"),
        P("section", "dp", "seq"),
        P("section", "dp", "seq"),
    )
    return jax.shard_map(
        shards,
        mesh=mesh,
        in_specs=placed,
        out_specs=P("section", "dp", "seq", None),
        check_vma=False,
    )
```

```python
import functools

import jax
import jax.numpy as jnp
from jax import lax
from jax.experimental import pallas as pl
from jax.experimental.pallas import tpu as pltpu
from jax.sharding import PartitionSpec as P

HEADS = 8
KV_HEADS = 4
HEAD_DIM = 256
DOC_MOST = 8
GROUP = HEADS // KV_HEADS

score_cap = 50.0
rope_base = 10000.0
log2_e = 1.4426950408889634


def shifted(block, axis, distance):
    count = lax.axis_size(axis)
    return lax.ppermute(block, axis, [(i, i + distance) for i in range(count - distance)])


def after(block, earlier):
    return lax.optimization_barrier((block, earlier))[0]


def passed_along(block, axis, distance):
    count = lax.axis_size(axis)
    return lax.ppermute(block, axis, [((i - distance) % count, i) for i in range(count)])


def pick_queries(flags_ref, source_ref, *out_refs):
    wide = GROUP * HEAD_DIM
    for g in range(KV_HEADS):
        out_refs[g][0] = source_ref[0, :, g * wide : (g + 1) * wide]


def pick_keys(flags_ref, source_ref, *out_refs):
    key_width = KV_HEADS * HEAD_DIM
    for g in range(KV_HEADS):
        begin = g * HEAD_DIM
        out_refs[g][0, :, :HEAD_DIM] = source_ref[0, :, begin : begin + HEAD_DIM]
        begin += key_width
        out_refs[g][0, :, HEAD_DIM:] = source_ref[0, :, begin : begin + HEAD_DIM]


def pick_blocks(kernel, flags, sources, capacity):
    blocks, rows, full_width = sources.shape
    column = 0 if kernel is pick_queries else 1

    def place(k, flags_ref):
        seen = jnp.int32(0)
        found = jnp.int32(0)
        for b in range(blocks):
            hit = flags_ref[b]
            found = jnp.where((hit == 1) & (seen == k), b, found)
            seen = seen + hit
        return (found, 0, column)

    width = full_width // 2
    each = width // KV_HEADS
    return pl.pallas_call(
        kernel,
        out_shape=[jax.ShapeDtypeStruct((capacity, rows, each), sources.dtype)] * KV_HEADS,
        grid_spec=pltpu.PrefetchScalarGridSpec(
            num_scalar_prefetch=1,
            grid=(capacity,),
            in_specs=[pl.BlockSpec((1, rows, width), place)],
            out_specs=[pl.BlockSpec((1, rows, each), lambda k, flags_ref: (k, 0, 0))] * KV_HEADS,
        ),
        cost_estimate=pl.CostEstimate(
            flops=0, bytes_accessed=2 * capacity * rows * width * 2, transcendentals=0
        ),
    )(flags, sources)


def attend_kernel(parts, blocks, extra, capacity, table_ref, *refs):
    q_refs = refs[:parts]
    own_refs = refs[parts : 2 * parts]
    prior_refs = refs[2 * parts : 3 * parts]
    extra_ref, cos_ref, sin_ref, out_ref, k_ref, v_ref, acc_ref, den_ref = refs[3 * parts :]
    rows = extra_ref.shape[1]
    half = HEAD_DIM // 2
    before = extra + blocks
    window = before + blocks
    pad = 1
    pos_at, first_at, live_at = window, 2 * window, 2 * window + blocks

    def turned(x, where):
        start = pl.multiple_of(where * rows, rows)
        c = cos_ref[pl.ds(start, rows), :]
        s = sin_ref[pl.ds(start, rows), :]
        x1 = x[:, :half].astype(jnp.float32)
        x2 = x[:, half:].astype(jnp.float32)
        return jnp.concatenate([x1 * c - x2 * s, x2 * c + x1 * s], axis=1).astype(jnp.bfloat16)

    def put(i, kv):
        begin = pl.multiple_of((i + pad) * rows, rows)
        k_ref[pl.ds(begin, rows), :] = turned(kv[:, :HEAD_DIM], table_ref[pos_at + i])
        v_ref[pl.ds(begin, rows), :] = kv[:, HEAD_DIM:]

    k_ref[pl.ds(0, rows), :] = jnp.zeros((rows, HEAD_DIM), jnp.bfloat16)
    v_ref[pl.ds(0, rows), :] = jnp.zeros((rows, HEAD_DIM), jnp.bfloat16)
    for i in range(extra):
        put(i, extra_ref[i])

    def chosen(part_refs, code, use):
        for n in range(parts):

            @pl.when((code >= n * capacity) & (code < (n + 1) * capacity))
            def _():
                use(part_refs[n][code - n * capacity])

    @pl.loop(extra, before)
    def _(i):
        chosen(prior_refs, table_ref[i], functools.partial(put, i))

    @pl.loop(before, window)
    def _(i):
        chosen(own_refs, table_ref[i], functools.partial(put, i))

    step = 2 * rows
    q_row = lax.broadcasted_iota(jnp.int32, (rows, step), 0)
    k_col = lax.broadcasted_iota(jnp.int32, (rows, step), 1)
    gap = k_col - q_row

    @pl.loop(0, blocks)
    def _(j):
        here = table_ref[pos_at + before + j]

        def run(q):
            q2 = jnp.concatenate(
                [turned(q[:, h * HEAD_DIM : (h + 1) * HEAD_DIM], here) for h in range(GROUP)], axis=0
            )
            acc_ref[...] = jnp.zeros_like(acc_ref)
            den_ref[...] = jnp.zeros_like(den_ref)
            first = table_ref[first_at + j]
            last = before + j

            @pl.loop(0, (last - first) // 2 + 1)
            def _(n):
                low = last - 1 - 2 * n
                begin = pl.multiple_of((low + pad) * rows, rows)
                k = k_ref[pl.ds(begin, step), :]
                v = v_ref[pl.ds(begin, step), :]
                s = lax.dot_general(
                    q2, k, (((1,), (1,)), ((), ())), preferred_element_type=jnp.float32
                )
                t = jnp.tanh(s * (HEAD_DIM**-0.5 / score_cap))
                w = jnp.exp2(t * (score_cap * log2_e))
                seen = (gap <= (last - low) * rows) & (k_col >= (first - low) * rows)
                seen = jnp.concatenate([seen] * GROUP, axis=0)
                w = jnp.where(seen, w, 0.0)
                den_ref[...] += w[:, :rows] + w[:, rows:]
                acc_ref[...] += jnp.dot(
                    w.astype(jnp.bfloat16), v, preferred_element_type=jnp.float32
                )

            total = jnp.sum(den_ref[...], axis=1, keepdims=True)
            mean = acc_ref[...] / total
            alive = (
                lax.broadcasted_iota(jnp.int32, (rows, HEAD_DIM), 0) < table_ref[live_at + j]
            )
            begin = pl.multiple_of(j * rows, rows)
            for h in range(GROUP):
                out_ref[pl.ds(begin, rows), h * HEAD_DIM : (h + 1) * HEAD_DIM] = jnp.where(
                    alive, mean[h * rows : (h + 1) * rows], 0.0
                ).astype(jnp.bfloat16)

        chosen(q_refs, table_ref[before + j], run)


def attend(table, queries, own, prior, beyond, cosine, sine):
    parts = len(queries)
    capacity, rows, wide = queries[0].shape
    blocks = parts * capacity
    extra = beyond.shape[0]
    window = extra + 2 * blocks
    spec = pl.BlockSpec(memory_space=pltpu.VMEM)
    pairs = blocks * (DOC_MOST // 2 + 1)
    return pl.pallas_call(
        functools.partial(attend_kernel, parts, blocks, extra, capacity),
        out_shape=jax.ShapeDtypeStruct((blocks * rows, wide), jnp.bfloat16),
        in_specs=[pl.BlockSpec(memory_space=pltpu.SMEM)] + [spec] * (3 * parts + 3),
        out_specs=spec,
        scratch_shapes=[
            pltpu.VMEM(((window + 1) * rows, HEAD_DIM), jnp.bfloat16),
            pltpu.VMEM(((window + 1) * rows, HEAD_DIM), jnp.bfloat16),
            pltpu.VMEM((GROUP * rows, HEAD_DIM), jnp.float32),
            pltpu.VMEM((GROUP * rows, rows), jnp.float32),
        ],
        cost_estimate=pl.CostEstimate(
            flops=pairs * 8 * GROUP * rows * rows * HEAD_DIM,
            bytes_accessed=4 * blocks * rows * wide * 2,
            transcendentals=pairs * 4 * GROUP * rows * rows,
        ),
    )(table, *queries, *own, *prior, beyond, cosine, sine)


def shards(projected, dest_owner, slot_from, doc_starts, live_rows):
    sources = projected[0, 0]
    blocks, rows, full_width = sources.shape
    dp_count = lax.axis_size("dp")
    capacity = (blocks + dp_count - 1) // dp_count
    owners = dest_owner[0, 0]
    numbers = slot_from[0, 0]
    starts = doc_starts[0, 0]
    me = lax.axis_index("dp")
    extra = DOC_MOST - 1 - blocks

    if dp_count == 2:
        mine = (owners == me).astype(jnp.int32)
        home_kv = list(pick_blocks(pick_keys, mine, sources, capacity))
        theirs, mine, home_kv[0] = lax.optimization_barrier((1 - mine, mine, home_kv[0]))
        away_kv = pick_blocks(pick_keys, theirs, sources, capacity)
        away_q = pick_blocks(pick_queries, theirs, sources, capacity)
        kvs, qs = [], []
        for g in range(KV_HEADS):
            kv, query = away_kv[g], away_q[g]
            if g >= 2:
                kv = after(kv, kvs[g - 2])
            if g >= 1:
                query = after(query, kvs[g - 1])
            kvs.append(passed_along(kv, "dp", 1))
            qs.append(passed_along(query, "dp", 1))
        home_q = pick_blocks(pick_queries, after(mine, kvs[0]), sources, capacity)
        heads = [((home_q[g], qs[g]), (home_kv[g], kvs[g])) for g in range(KV_HEADS)]
        codes = numbers % capacity + jnp.where(numbers // capacity == me, 0, capacity)
    else:
        earlier = jnp.tril(jnp.ones((blocks, blocks), jnp.int32), -1)
        rank = jnp.sum((owners[:, None] == owners[None, :]) * earlier, axis=1)
        target = owners * capacity + rank
        hits = target[None, :] == jnp.arange(dp_count * capacity)[:, None]
        order = jnp.sum(jnp.where(hits, jnp.arange(blocks)[None, :], 0), axis=1)
        got = lax.all_to_all(
            jnp.take(sources, order, axis=0), "dp", split_axis=0, concat_axis=0, tiled=True
        )
        packed = jnp.take(got, numbers, axis=0)
        every = jnp.ones((blocks,), jnp.int32)
        queries = pick_blocks(pick_queries, every, packed, blocks)
        keys = pick_blocks(pick_keys, every, packed, blocks)
        heads = [((queries[g],), (keys[g],)) for g in range(KV_HEADS)]
        codes = jnp.arange(blocks, dtype=jnp.int32)

    codes, starts, _ = lax.optimization_barrier((codes, starts, heads[0][1][-1]))
    both = jnp.concatenate([codes, starts]).astype(jnp.int32)
    below = shifted(both, "seq", 1)
    beneath = shifted(starts, "seq", 2)
    flags = jnp.concatenate([beneath[blocks - extra :], below[blocks:], starts])
    window = extra + 2 * blocks
    ids = jnp.arange(window, dtype=jnp.int32)
    before = extra + blocks
    opened = (flags[None, :] == 1) & (ids[None, :] <= ids[:, None])
    first = jnp.max(jnp.where(opened, ids[None, :], 0), axis=1)
    at_start = first[before]
    position = jnp.where(ids < before, ids - at_start, ids - first)
    position = jnp.clip(position, 0, DOC_MOST - 1)
    table = jnp.concatenate(
        [
            jnp.zeros((extra,), jnp.int32),
            below[:blocks],
            codes.astype(jnp.int32),
            position,
            first[before:],
            live_rows[0, 0],
        ]
    )

    half = HEAD_DIM // 2
    frequency = rope_base ** (-2.0 * jnp.arange(half, dtype=jnp.float32) / HEAD_DIM)
    places = jnp.arange(DOC_MOST * rows, dtype=jnp.float32)
    places, _ = lax.optimization_barrier((places, heads[0][1][-1]))
    angles = places[:, None] * frequency[None, :]
    cosine, sine = jnp.cos(angles), jnp.sin(angles)

    def tail(kv, codes):
        picked = []
        for e in range(extra):
            code = codes[blocks - extra + e]
            size = kv[0].shape[0]
            best = lax.dynamic_slice_in_dim(kv[0], jnp.clip(code, 0, size - 1), 1, 0)
            for n in range(1, len(kv)):
                other = lax.dynamic_slice_in_dim(
                    kv[n], jnp.clip(code - n * size, 0, size - 1), 1, 0
                )
                best = jnp.where(code >= n * size, other, best)
            picked.append(best)
        return jnp.concatenate(picked)

    priors = []
    for g, (queries, kv) in enumerate(heads):
        kv = list(kv)
        if len(kv) == 2:
            if g == 2:
                kv[0] = after(kv[0], heads[0][1][1])
            if g == 3:
                kv[0] = after(kv[0], priors[0][1])
            if g >= 2:
                kv[1] = after(kv[1], priors[g - 2][1])
        priors.append(tuple(shifted(part, "seq", 1) for part in kv))
    handed = []
    for g, (queries, kv) in enumerate(heads):
        beyond = shifted(tail(priors[g], below[:blocks]), "seq", 1)
        out = attend(table, queries, kv, priors[g], beyond, cosine, sine)
        handed.append(passed_along(out, "section", 1))
    return jnp.concatenate(handed, axis=1)[None, None]


def solution(mesh):
    placed = (
        P("section", "seq", "dp", None, None),
        P("section", "seq", "dp"),
        P("section", "dp", "seq"),
        P("section", "dp", "seq"),
        P("section", "dp", "seq"),
    )
    return jax.shard_map(
        shards,
        mesh=mesh,
        in_specs=placed,
        out_specs=P("section", "dp", "seq", None),
        check_vma=False,
    )
```

```python
import functools

import jax
import jax.numpy as jnp
from jax import lax
from jax.experimental import pallas as pl
from jax.experimental.pallas import tpu as pltpu
from jax.sharding import PartitionSpec as P

HEADS = 8
KV_HEADS = 4
HEAD_DIM = 256
DOC_MOST = 8
GROUP = HEADS // KV_HEADS

score_cap = 50.0
rope_base = 10000.0
log2_e = 1.4426950408889634


def shifted(block, axis, distance):
    count = lax.axis_size(axis)
    return lax.ppermute(block, axis, [(i, i + distance) for i in range(count - distance)])


def passed_along(block, axis, distance):
    count = lax.axis_size(axis)
    return lax.ppermute(block, axis, [((i - distance) % count, i) for i in range(count)])


def pick_queries(flags_ref, source_ref, *out_refs):
    wide = GROUP * HEAD_DIM
    for g in range(KV_HEADS):
        out_refs[g][0] = source_ref[0, :, g * wide : (g + 1) * wide]


def pick_keys(flags_ref, source_ref, *out_refs):
    key_width = KV_HEADS * HEAD_DIM
    for g in range(KV_HEADS):
        begin = g * HEAD_DIM
        out_refs[g][0, :, :HEAD_DIM] = source_ref[0, :, begin : begin + HEAD_DIM]
        begin += key_width
        out_refs[g][0, :, HEAD_DIM:] = source_ref[0, :, begin : begin + HEAD_DIM]


def pick_blocks(kernel, flags, sources, capacity):
    blocks, rows, full_width = sources.shape
    column = 0 if kernel is pick_queries else 1

    def place(k, flags_ref):
        seen = jnp.int32(0)
        found = jnp.int32(0)
        for b in range(blocks):
            hit = flags_ref[b]
            found = jnp.where((hit == 1) & (seen == k), b, found)
            seen = seen + hit
        return (found, 0, column)

    width = full_width // 2
    each = width // KV_HEADS
    return pl.pallas_call(
        kernel,
        out_shape=[jax.ShapeDtypeStruct((capacity, rows, each), sources.dtype)] * KV_HEADS,
        grid_spec=pltpu.PrefetchScalarGridSpec(
            num_scalar_prefetch=1,
            grid=(capacity,),
            in_specs=[pl.BlockSpec((1, rows, width), place)],
            out_specs=[pl.BlockSpec((1, rows, each), lambda k, flags_ref: (k, 0, 0))] * KV_HEADS,
        ),
        cost_estimate=pl.CostEstimate(
            flops=0, bytes_accessed=2 * capacity * rows * width * 2, transcendentals=0
        ),
    )(flags, sources)


def attend_kernel(parts, blocks, extra, capacity, table_ref, *refs):
    q_refs = refs[:parts]
    own_refs = refs[parts : 2 * parts]
    prior_refs = refs[2 * parts : 3 * parts]
    extra_ref, cos_ref, sin_ref, out_ref, k_ref, v_ref, q_ref, acc_ref, den_ref = refs[3 * parts :]
    rows = extra_ref.shape[1]
    half = HEAD_DIM // 2
    before = extra + blocks
    window = before + blocks
    pad = 1
    pos_at, first_at, live_at = window, 2 * window, 2 * window + blocks

    def turned(x, where):
        start = pl.multiple_of(where * rows, rows)
        c = cos_ref[pl.ds(start, rows), :]
        s = sin_ref[pl.ds(start, rows), :]
        x1 = x[:, :half].astype(jnp.float32)
        x2 = x[:, half:].astype(jnp.float32)
        return jnp.concatenate([x1 * c - x2 * s, x2 * c + x1 * s], axis=1).astype(jnp.bfloat16)

    def put(i, kv):
        begin = pl.multiple_of((i + pad) * rows, rows)
        k_ref[pl.ds(begin, rows), :] = turned(kv[:, :HEAD_DIM], table_ref[pos_at + i])
        v_ref[pl.ds(begin, rows), :] = kv[:, HEAD_DIM:]

    k_ref[pl.ds(0, rows), :] = jnp.zeros((rows, HEAD_DIM), jnp.bfloat16)
    v_ref[pl.ds(0, rows), :] = jnp.zeros((rows, HEAD_DIM), jnp.bfloat16)
    for i in range(extra):
        put(i, extra_ref[i])

    def chosen(part_refs, code, use):
        for n in range(parts):

            @pl.when((code >= n * capacity) & (code < (n + 1) * capacity))
            def _():
                use(part_refs[n][code - n * capacity])

    @pl.loop(extra, before)
    def _(i):
        chosen(prior_refs, table_ref[i], functools.partial(put, i))

    @pl.loop(before, window)
    def _(i):
        chosen(own_refs, table_ref[i], functools.partial(put, i))

    step = 2 * rows
    pair = 2 if blocks % 2 == 0 else 1
    tall = pair * rows
    q_row = lax.broadcasted_iota(jnp.int32, (tall, step), 0)
    k_col = lax.broadcasted_iota(jnp.int32, (tall, step), 1)
    gap = k_col - q_row
    row = lax.broadcasted_iota(jnp.int32, (tall, 1), 0)

    def stage(j, q):
        here = table_ref[pos_at + before + j]
        u = lax.rem(j, pair)
        for h in range(GROUP):
            begin = pl.multiple_of(h * tall + u * rows, rows)
            q_ref[pl.ds(begin, rows), :] = turned(q[:, h * HEAD_DIM : (h + 1) * HEAD_DIM], here)

    @pl.loop(0, blocks // pair)
    def _(m):
        base = m * pair
        for u in range(pair):
            chosen(q_refs, table_ref[before + base + u], functools.partial(stage, base + u))
        acc_ref[...] = jnp.zeros_like(acc_ref)
        den_ref[...] = jnp.zeros_like(den_ref)
        first = table_ref[first_at + base]
        lowest = jnp.where(row < rows, first, table_ref[first_at + base + pair - 1])
        last = before + base + pair - 1

        @pl.loop(0, (last - first) // 2 + 1)
        def _(n):
            low = last - 1 - 2 * n
            begin = pl.multiple_of((low + pad) * rows, rows)
            k = k_ref[pl.ds(begin, step), :]
            v = v_ref[pl.ds(begin, step), :]
            seen = (gap <= (before + base - low) * rows) & (k_col >= (lowest - low) * rows)
            for h in range(GROUP):
                part = pl.ds(h * tall, tall)
                s = lax.dot_general(
                    q_ref[part, :], k, (((1,), (1,)), ((), ())), preferred_element_type=jnp.float32
                )
                t = jnp.tanh(s * (HEAD_DIM**-0.5 / score_cap))
                w = jnp.where(seen, jnp.exp2(t * (score_cap * log2_e)), 0.0)
                den_ref[part, :] += w[:, :rows] + w[:, rows:]
                acc_ref[part, :] += jnp.dot(
                    w.astype(jnp.bfloat16), v, preferred_element_type=jnp.float32
                )

        total = jnp.sum(den_ref[...], axis=1, keepdims=True)
        mean = acc_ref[...] * (1.0 / total)
        ends = jnp.where(row < rows, table_ref[live_at + base], 0)
        if pair == 2:
            ends = jnp.where(row < rows, ends, table_ref[live_at + base + 1] + rows)
        begin = pl.multiple_of(base * rows, rows)
        for h in range(GROUP):
            out_ref[pl.ds(begin, tall), h * HEAD_DIM : (h + 1) * HEAD_DIM] = jnp.where(
                row < ends, mean[h * tall : (h + 1) * tall], 0.0
            ).astype(jnp.bfloat16)


def attend(table, queries, own, prior, beyond, cosine, sine):
    parts = len(queries)
    capacity, rows, wide = queries[0].shape
    blocks = parts * capacity
    extra = beyond.shape[0]
    window = extra + 2 * blocks
    spec = pl.BlockSpec(memory_space=pltpu.VMEM)
    pair = 2 if blocks % 2 == 0 else 1
    pairs = blocks * (DOC_MOST // 2 + 1)
    return pl.pallas_call(
        functools.partial(attend_kernel, parts, blocks, extra, capacity),
        out_shape=jax.ShapeDtypeStruct((blocks * rows, wide), jnp.bfloat16),
        in_specs=[pl.BlockSpec(memory_space=pltpu.SMEM)] + [spec] * (3 * parts + 3),
        out_specs=spec,
        scratch_shapes=[
            pltpu.VMEM(((window + 1) * rows, HEAD_DIM), jnp.bfloat16),
            pltpu.VMEM(((window + 1) * rows, HEAD_DIM), jnp.bfloat16),
            pltpu.VMEM((pair * GROUP * rows, HEAD_DIM), jnp.bfloat16),
            pltpu.VMEM((pair * GROUP * rows, HEAD_DIM), jnp.float32),
            pltpu.VMEM((pair * GROUP * rows, rows), jnp.float32),
        ],
        cost_estimate=pl.CostEstimate(
            flops=pairs * 8 * GROUP * rows * rows * HEAD_DIM,
            bytes_accessed=4 * blocks * rows * wide * 2,
            transcendentals=pairs * 4 * GROUP * rows * rows,
        ),
    )(table, *queries, *own, *prior, beyond, cosine, sine)


def shards(projected, dest_owner, slot_from, doc_starts, live_rows):
    sources = projected[0, 0]
    blocks, rows, full_width = sources.shape
    dp_count = lax.axis_size("dp")
    capacity = (blocks + dp_count - 1) // dp_count
    owners = dest_owner[0, 0]
    numbers = slot_from[0, 0]
    starts = doc_starts[0, 0]
    me = lax.axis_index("dp")
    extra = DOC_MOST - 1 - blocks

    if dp_count == 2:
        mine = (owners == me).astype(jnp.int32)
        home_kv = list(pick_blocks(pick_keys, mine, sources, capacity))
        theirs, mine, home_kv[0] = lax.optimization_barrier((1 - mine, mine, home_kv[0]))
        away_kv = pick_blocks(pick_keys, theirs, sources, capacity)
        away_q = pick_blocks(pick_queries, theirs, sources, capacity)
        home_q = pick_blocks(pick_queries, mine, sources, capacity)
        heads = []
        for g in range(KV_HEADS):
            kv = passed_along(away_kv[g], "dp", 1)
            kv, query = lax.optimization_barrier((kv, away_q[g]))
            query = passed_along(query, "dp", 1)
            heads.append(((home_q[g], query), (home_kv[g], kv)))
        codes = numbers % capacity + jnp.where(numbers // capacity == me, 0, capacity)
    else:
        earlier = jnp.tril(jnp.ones((blocks, blocks), jnp.int32), -1)
        rank = jnp.sum((owners[:, None] == owners[None, :]) * earlier, axis=1)
        target = owners * capacity + rank
        hits = target[None, :] == jnp.arange(dp_count * capacity)[:, None]
        order = jnp.sum(jnp.where(hits, jnp.arange(blocks)[None, :], 0), axis=1)
        got = lax.all_to_all(
            jnp.take(sources, order, axis=0), "dp", split_axis=0, concat_axis=0, tiled=True
        )
        packed = jnp.take(got, numbers, axis=0)
        every = jnp.ones((blocks,), jnp.int32)
        away_kv = [every]
        queries = pick_blocks(pick_queries, every, packed, blocks)
        keys = pick_blocks(pick_keys, every, packed, blocks)
        heads = [((queries[g],), (keys[g],)) for g in range(KV_HEADS)]
        codes = jnp.arange(blocks, dtype=jnp.int32)

    codes, starts, _ = lax.optimization_barrier((codes, starts, away_kv[0]))
    both = jnp.concatenate([codes, starts]).astype(jnp.int32)
    below = shifted(both, "seq", 1)
    beneath = shifted(starts, "seq", 2)
    flags = jnp.concatenate([beneath[blocks - extra :], below[blocks:], starts])
    window = extra + 2 * blocks
    ids = jnp.arange(window, dtype=jnp.int32)
    before = extra + blocks
    opened = (flags[None, :] == 1) & (ids[None, :] <= ids[:, None])
    first = jnp.max(jnp.where(opened, ids[None, :], 0), axis=1)
    at_start = first[before]
    position = jnp.where(ids < before, ids - at_start, ids - first)
    position = jnp.clip(position, 0, DOC_MOST - 1)
    table = jnp.concatenate(
        [
            jnp.zeros((extra,), jnp.int32),
            below[:blocks],
            codes.astype(jnp.int32),
            position,
            first[before:],
            live_rows[0, 0],
        ]
    )

    half = HEAD_DIM // 2
    frequency = rope_base ** (-2.0 * jnp.arange(half, dtype=jnp.float32) / HEAD_DIM)
    angles = jnp.arange(DOC_MOST * rows, dtype=jnp.float32)[:, None] * frequency[None, :]
    cosine, sine = jnp.cos(angles), jnp.sin(angles)

    def tail(kv, codes):
        picked = []
        for e in range(extra):
            code = codes[blocks - extra + e]
            size = kv[0].shape[0]
            best = lax.dynamic_slice_in_dim(kv[0], jnp.clip(code, 0, size - 1), 1, 0)
            for n in range(1, len(kv)):
                other = lax.dynamic_slice_in_dim(
                    kv[n], jnp.clip(code - n * size, 0, size - 1), 1, 0
                )
                best = jnp.where(code >= n * size, other, best)
            picked.append(best)
        return jnp.concatenate(picked)

    def after(block, *earlier):
        return lax.optimization_barrier((block, *earlier))[0]

    priors = []
    for g, (queries, kv) in enumerate(heads):
        kv = list(kv)
        if len(kv) == 2:
            if g == 2:
                kv[0] = after(kv[0], heads[0][1][1])
            if g == 3:
                kv[0] = after(kv[0], priors[0][1])
            if g >= 2:
                kv[1] = after(kv[1], priors[g - 2][1])
        priors.append(tuple(shifted(part, "seq", 1) for part in kv))
    handed = []
    for g, (queries, kv) in enumerate(heads):
        beyond = shifted(tail(priors[g], below[:blocks]), "seq", 1)
        out = attend(table, queries, kv, priors[g], beyond, cosine, sine)
        handed.append(passed_along(out, "section", 1))
    return jnp.concatenate(handed, axis=1)[None, None]


def solution(mesh):
    placed = (
        P("section", "seq", "dp", None, None),
        P("section", "seq", "dp"),
        P("section", "dp", "seq"),
        P("section", "dp", "seq"),
        P("section", "dp", "seq"),
    )
    return jax.shard_map(
        shards,
        mesh=mesh,
        in_specs=placed,
        out_specs=P("section", "dp", "seq", None),
        check_vma=False,
    )
```
